32 devices in a mesh: blk: 8 (over z, x), tile: 4 (over y, core).
Axes of the slice: x: 2, y: 2, z: 4, core: 2. Of those that a mesh axis runs over, the one named last changes fastest.
Arguments:
- stream_in: bfloat16 [32, 16, 16, 2240], P('tile', 'blk'), may hold values from -6 to 6
- queries: bfloat16 [32, 16, 16, 2240], P('tile', 'blk'), may hold values from -12 to 12
- key_rows: bfloat16 [32, 16, 16, 2240], P('tile', 'blk'), may hold values from -12 to 12
- value_rows: bfloat16 [32, 16, 16, 2240], P('tile', 'blk'), may hold values from -12 to 12
- w_output: bfloat16 [2240, 2240], P('tile'), may hold values from -0.125 to 0.125
- w_inner: bfloat16 [2240, 2, 4096], P(None, None, 'tile'), may hold values from -0.125 to 0.125
- w_down: bfloat16 [4096, 2240], P('tile'), may hold values from -0.09375 to 0.09375
- spatial_taps: float32 [3, 3, 2, 4096], P(None, None, None, 'tile'), may hold values from -2 to 2
- temporal_taps: float32 [3, 2, 4096], P(None, None, 'tile'), may hold values from -3.5 to 3.5
Outputs:
- layer_out: bfloat16 [32, 16, 16, 2240], P('tile', 'blk')
The draws below stay inside these ranges and needn't reach their ends.
All inputs are finite; a program needn't handle non-finite values.
Results may differ from the reference program's by a relative error of at most 0.009.
Values may be sent and summed in bfloat16 or wider, within the bound.
A program may use at most 128 MiB of HBM per device.

```python
import jax
import jax.numpy as jnp
from jax import lax

HEADS = 20
HEAD_DIM = 112
D = 2240
FF_WIN = 4096
ROWS = 32
COLS = 16
BLOCK_F = 4
TAPS = 3
FRAMES = 16


def cluster_tables(key):
    mask_key = jax.random.fold_in(key, 101)
    magnitude_key = jax.random.fold_in(key, 102)
    value_key = jax.random.fold_in(key, 103)
    active = jax.random.bernoulli(mask_key, 0.12, (HEADS, HEAD_DIM, HEAD_DIM))
    own_channel = jnp.eye(HEAD_DIM, dtype=jnp.float32)[None] > 0.5
    active = jnp.logical_or(active, own_channel)
    magnitude = jnp.exp(jax.random.uniform(magnitude_key, (HEADS, HEAD_DIM, HEAD_DIM), jnp.float32, 0.405, 1.386))
    proto_key = jnp.where(active, magnitude, 0.0)
    proto_value = 2.0 * jax.random.normal(value_key, (HEADS, HEAD_DIM, HEAD_DIM), jnp.float32)
    return (proto_key, proto_value)


def token_noise(noise_key):
    shape_heads = (ROWS, FRAMES, COLS, HEADS, HEAD_DIM)
    return jax.random.normal(noise_key, shape_heads, jnp.float32)


def pick_rows(table, clusters):
    head_index = jnp.arange(HEADS, dtype=jnp.int32)
    return table[head_index, clusters]


def positive_rows(key, salt):
    proto_key, proto_value = cluster_tables(key)
    clusters = jax.random.randint(jax.random.fold_in(key, salt), (ROWS, FRAMES, COLS, HEADS), 0, HEAD_DIM)
    gain = jnp.exp(jax.random.uniform(jax.random.fold_in(key, salt + 1), (ROWS, FRAMES, COLS, HEADS, 1), jnp.float32, -1.5, 1.5))
    noise = token_noise(jax.random.fold_in(key, salt + 2))
    rows = gain * (pick_rows(proto_key, clusters) + 0.3 * noise)
    return (rows, clusters, proto_value)


def draw_queries(key, part):
    rows, clusters, proto_value = positive_rows(key, 211)
    return jnp.clip(rows, -12.0, 12.0).reshape(ROWS, FRAMES, COLS, D).astype(jnp.bfloat16)


def draw_key_rows(key, part):
    rows, clusters, proto_value = positive_rows(key, 311)
    return jnp.clip(rows, -12.0, 12.0).reshape(ROWS, FRAMES, COLS, D).astype(jnp.bfloat16)


def draw_value_rows(key, part):
    rows, clusters, proto_value = positive_rows(key, 311)
    noise = token_noise(jax.random.fold_in(key, 411))
    offset = 2.0 * jax.random.normal(jax.random.fold_in(key, 412), (1, FRAMES, 1, HEADS, HEAD_DIM), jnp.float32)
    values = noise + pick_rows(proto_value, clusters) + offset
    return jnp.clip(values, -12.0, 12.0).reshape(ROWS, FRAMES, COLS, D).astype(jnp.bfloat16)


def level_of(rng, dims, shards, low, largest):
    def one(position, parts):
        steps = jax.random.uniform(jax.random.fold_in(jax.random.fold_in(rng, 6), position), (parts,), jnp.float32, low / len(shards), largest / len(shards))
        return jnp.repeat(jnp.exp(steps), dims[position] // parts).reshape((-1,) + (1,) * (len(dims) - position - 1))

    factor_of = one(*shards[0])
    for cut in shards[1:]:
        factor_of = factor_of * one(*cut)
    return factor_of


def gaussian(rng, shape, width, bound, cuts=(), held_as=jnp.bfloat16):
    values = jax.random.normal(rng, shape, jnp.float32) * width
    if len(cuts) > 0:
        values = level_of(rng, shape, cuts, -0.22, 0.18) * values
    return jnp.clip(values, min=-bound, max=bound).astype(held_as)


def setup_inputs(seed: int = 0) -> dict:
    key_of = jax.random.split(jax.random.key(seed), 10)
    return {
        "stream_in": gaussian(key_of[0], (ROWS, FRAMES, COLS, D), 1.0, 6.0, ((0, 4), (1, 8))),
        "queries": draw_queries(jax.random.fold_in(key_of[9], 71), 0),
        "key_rows": draw_key_rows(jax.random.fold_in(key_of[9], 71), 0),
        "value_rows": draw_value_rows(jax.random.fold_in(key_of[9], 71), 0),
        "w_output": gaussian(key_of[4], (D, D), D ** -0.5, 0.125, ((0, 4),)),
        "w_inner": gaussian(key_of[5], (D, 2, FF_WIN), D ** -0.5, 0.125, ((2, 4),)),
        "w_down": gaussian(key_of[6], (FF_WIN, D), FF_WIN ** -0.5, 0.09375, ((0, 4),)),
        "spatial_taps": gaussian(key_of[7], (3, 3, 2, FF_WIN), 9 ** -0.5, 2.0, ((3, 4),), jnp.float32),
        "temporal_taps": gaussian(key_of[8], (TAPS, 2, FF_WIN), TAPS ** -0.5, 3.5, ((2, 4),), jnp.float32),
    }


EPS = 1e-6


def spatial_conv(inner_act, spatial_taps):
    row_count = inner_act.shape[0]
    col_count = inner_act.shape[2]
    padded = jnp.pad(inner_act, ((1, 1), (0, 0), (1, 1), (0, 0), (0, 0)))
    running = jnp.zeros(inner_act.shape, jnp.float32)
    for tap_row in range(3):
        for tap_col in range(3):
            window = padded[tap_row:tap_row + row_count, :, tap_col:tap_col + col_count]
            running = running + window.astype(jnp.float32) * spatial_taps[tap_row, tap_col]
    return running


def reference(stream_in, queries, key_rows, value_rows, w_output, w_inner, w_down, spatial_taps, temporal_taps):
    highest = lax.Precision.HIGHEST
    shape_heads = (ROWS, FRAMES, COLS, HEADS, HEAD_DIM)
    query_pos = jax.nn.relu(queries.astype(jnp.float32)).reshape(shape_heads)
    key_pos = jax.nn.relu(key_rows.astype(jnp.float32)).reshape(shape_heads)
    values = value_rows.astype(jnp.float32).reshape(shape_heads)
    frame_kv = jnp.einsum('rfchd,rfche->fhde', key_pos, values, precision=highest)
    frame_z = jnp.sum(key_pos, axis=(0, 2))
    block_count = FRAMES // BLOCK_F
    block_kv = frame_kv.reshape(block_count, BLOCK_F, HEADS, HEAD_DIM, HEAD_DIM).sum(1)
    block_z = frame_z.reshape(block_count, BLOCK_F, HEADS, HEAD_DIM).sum(1)
    state = jnp.repeat(jnp.cumsum(block_kv, 0), BLOCK_F, axis=0)
    zsum = jnp.repeat(jnp.cumsum(block_z, 0), BLOCK_F, axis=0)
    numerator = jnp.einsum('rfchd,fhde->rfche', query_pos, state, precision=highest)
    denominator = jnp.einsum('rfchd,fhd->rfch', query_pos, zsum, precision=highest) + EPS
    attended = (numerator / denominator[..., None]).reshape(ROWS * FRAMES * COLS, D).astype(jnp.bfloat16)
    attn_out = jnp.dot(attended, w_output, preferred_element_type=jnp.float32)
    hidden = (stream_in.astype(jnp.float32).reshape(-1, D) + attn_out).astype(jnp.bfloat16)
    inner_act = jax.nn.silu(jnp.dot(hidden, w_inner.reshape(D, 2 * FF_WIN), preferred_element_type=jnp.float32))
    inner_act = inner_act.astype(jnp.bfloat16).reshape(ROWS, FRAMES, COLS, 2, FF_WIN)
    spatial = spatial_conv(inner_act, spatial_taps).astype(jnp.bfloat16)
    extended = jnp.pad(spatial, ((0, 0), (TAPS - 1, 0), (0, 0), (0, 0), (0, 0)))
    temporal_mix = jnp.zeros(spatial.shape, jnp.float32)
    for lag in range(TAPS):
        window = extended[:, TAPS - 1 - lag:TAPS - 1 - lag + FRAMES]
        temporal_mix = temporal_mix + window.astype(jnp.float32) * temporal_taps[lag]
    gated_out = (temporal_mix[..., 0, :] * jax.nn.silu(temporal_mix[..., 1, :])).astype(jnp.bfloat16)
    ffn_out = jnp.dot(gated_out.reshape(-1, FF_WIN), w_down, preferred_element_type=jnp.float32)
    layer_out = (hidden.astype(jnp.float32) + ffn_out).astype(jnp.bfloat16)
    return layer_out.reshape(ROWS, FRAMES, COLS, D)
```

```python
import functools

import jax
import jax.numpy as jnp
from jax import lax
from jax.experimental import pallas as pl
from jax.experimental.pallas import tpu as pltpu
from jax.sharding import PartitionSpec as P

HEADS = 20
HEAD_DIM = 112
TAPS = 3
BLOCK_F = 4
LANES = 128
EPS = 1e-06

MESH = pl.DeviceIdType.MESH


def vmem_specs(count):
    return [pl.BlockSpec(memory_space=pltpu.VMEM)] * count


def shifted(x, axis, by):
    peers = lax.axis_size(axis)
    pairs = [(i, i + by) for i in range(peers) if 0 <= i + by < peers]
    return lax.ppermute(x, axis, pairs)


def head_columns(head):
    return slice(head * HEAD_DIM, (head + 1) * HEAD_DIM)


def local_state_kernel(key_ref, value_ref, kv_ref):
    tokens = key_ref.shape[0]
    ones = jnp.ones((tokens, LANES - HEAD_DIM), jnp.bfloat16)
    for head in range(HEADS):
        keys = jnp.maximum(key_ref[:, head_columns(head)], 0)
        values = jnp.concatenate([value_ref[:, head_columns(head)], ones], axis=1)
        kv = lax.dot_general(
            keys, values, (((0,), (0,)), ((), ())), preferred_element_type=jnp.float32
        )
        kv_ref[head] = kv.astype(jnp.bfloat16)
    for head in range(HEADS, kv_ref.shape[0]):
        kv_ref[head] = jnp.zeros(kv_ref.shape[1:], jnp.bfloat16)


def exchange_kernel(
    blocks, pair, tiles, kv_ref, state_ref, got1, got2, total, block_send, final_send, states,
    send1, recv1, send2, recv2, send3, recv3,
):
    group = pair * tiles
    blk = lax.axis_index("blk")
    tile = lax.axis_index("tile")
    block = blk // pair
    member = blk % pair
    rank = member * tiles + tile

    def peer(step):
        other = (rank + step) % group
        return other, (block * pair + other // tiles, other % tiles)

    barrier = pltpu.get_barrier_semaphore()
    for step in range(1, group):
        pl.semaphore_signal(barrier, inc=1, device_id=peer(step)[1], device_id_type=MESH)
    for step in range(1, blocks):
        other = (block + step) % blocks
        pl.semaphore_signal(
            barrier, inc=1, device_id=(other * pair + member, tile), device_id_type=MESH
        )
    pl.semaphore_wait(barrier, group - 1 + blocks - 1)

    first = []
    for step in range(1, group):
        other, device = peer(step)
        copy = pltpu.make_async_remote_copy(
            src_ref=kv_ref.at[other], dst_ref=got1.at[step], send_sem=send1.at[step],
            recv_sem=recv1.at[step], device_id=device, device_id_type=MESH,
        )
        copy.start()
        first.append(copy)
    total[...] = kv_ref[rank].astype(jnp.float32)
    for step in range(1, group):
        first[step - 1].wait_recv()
        total[...] += got1[step].astype(jnp.float32)

    block_send[...] = total[...].astype(jnp.bfloat16)

    def later(step):
        return pltpu.make_async_remote_copy(
            src_ref=block_send, dst_ref=got2.at[step], send_sem=send2.at[step],
            recv_sem=recv2.at[step], device_id=(((block + step) % blocks) * pair + member, tile),
            device_id_type=MESH,
        )

    for step in range(1, blocks):

        @pl.when(block + step < blocks)
        def _():
            later(step).start()

    for step in range(1, blocks):

        @pl.when(block >= step)
        def _():
            later(step).wait_recv()
            total[...] += got2[step].astype(jnp.float32)

    final_send[...] = total[...].astype(jnp.bfloat16)
    third = []
    for step in range(1, group):
        copy = pltpu.make_async_remote_copy(
            src_ref=final_send, dst_ref=states.at[rank], send_sem=send3.at[step],
            recv_sem=recv3.at[step], device_id=peer(step)[1], device_id_type=MESH,
        )
        copy.start()
        third.append(copy)
    state_ref[rank] = total[...].astype(jnp.bfloat16)
    for step in range(1, group):
        third[step - 1].wait_recv()
        other = (rank + group - step) % group
        state_ref[other] = states[other]
    for step in range(1, group):
        first[step - 1].wait_send()
        third[step - 1].wait_send()
    for step in range(1, blocks):

        @pl.when(block + step < blocks)
        def _():
            later(step).wait_send()


def exchange_states(kv, blocks, pair, tiles):
    group = pair * tiles
    piece = kv.shape[1:]
    dma = pltpu.SemaphoreType.DMA
    return pl.pallas_call(
        functools.partial(exchange_kernel, blocks, pair, tiles),
        out_shape=jax.ShapeDtypeStruct(kv.shape, jnp.bfloat16),
        in_specs=vmem_specs(1),
        out_specs=vmem_specs(1)[0],
        scratch_shapes=[
            pltpu.VMEM((group,) + piece, jnp.bfloat16),
            pltpu.VMEM((blocks,) + piece, jnp.bfloat16),
            pltpu.VMEM(piece, jnp.float32),
            pltpu.VMEM(piece, jnp.bfloat16),
            pltpu.VMEM(piece, jnp.bfloat16),
            pltpu.VMEM((group,) + piece, jnp.bfloat16),
            dma((group,)),
            dma((group,)),
            dma((blocks,)),
            dma((blocks,)),
            dma((group,)),
            dma((group,)),
        ],
        compiler_params=pltpu.CompilerParams(collective_id=0, has_side_effects=True),
    )(kv)


def attention_kernel(query_ref, state_ref, out_ref):
    for head in range(HEADS):
        queries = jnp.maximum(query_ref[:, head_columns(head)], 0)
        both = jnp.dot(queries, state_ref[head], preferred_element_type=jnp.float32)
        ratio = both[:, :HEAD_DIM] / (both[:, HEAD_DIM : HEAD_DIM + 1] + EPS)
        out_ref[:, head_columns(head)] = ratio.astype(jnp.bfloat16)


def column_masks(stride, cols, width):
    col = lax.broadcasted_iota(jnp.int32, (stride, width), 0) % cols
    return col > 0, col < cols - 1


def fill_inner(hidden_ref, w_ref, inner, stride, chunk):
    tokens = hidden_ref.shape[0]
    edge = jnp.zeros((stride, inner.shape[1]), jnp.bfloat16)
    inner[:stride] = edge
    inner[stride + tokens :] = edge
    for start in range(0, tokens, chunk):
        product = jnp.dot(
            hidden_ref[start : start + chunk], w_ref[...], preferred_element_type=jnp.float32
        )
        inner[stride + start : stride + start + chunk] = jax.nn.silu(product).astype(jnp.bfloat16)


def conv_row(inner, taps_ref, row, stride, masks):
    rows = [
        inner[pl.ds(pl.multiple_of((row + a) * stride, stride), stride)].astype(jnp.float32)
        for a in range(3)
    ]
    sums = [
        sum(rows[a] * taps_ref[3 * a + b : 3 * a + b + 1] for a in range(3)) for b in range(3)
    ]
    from_left = jnp.where(masks[0], pltpu.roll(sums[0], 1, 0), 0.0)
    from_right = jnp.where(masks[1], pltpu.roll(sums[2], stride - 1, 0), 0.0)
    return sums[1] + from_left + from_right


def spatial_kernel(stride, cols, chunk, hidden_ref, w_ref, taps_ref, out_ref, inner):
    fill_inner(hidden_ref, w_ref, inner, stride, chunk)
    masks = column_masks(stride, cols, inner.shape[1])

    def body(row, carry):
        value = conv_row(inner, taps_ref, row, stride, masks)
        out_ref[pl.ds(pl.multiple_of(row * stride, stride), stride)] = value.astype(jnp.bfloat16)
        return carry

    lax.fori_loop(0, hidden_ref.shape[0] // stride, body, 0, unroll=2)


def gated_kernel(
    stride, cols, chunk, hidden_ref, wv_ref, wg_ref, sv_ref, sg_ref, tv_ref, tg_ref, ov_ref, og_ref,
    out_ref, inner_v, inner_g,
):
    fill_inner(hidden_ref, wv_ref, inner_v, stride, chunk)
    fill_inner(hidden_ref, wg_ref, inner_g, stride, chunk)
    masks = column_masks(stride, cols, inner_v.shape[1])

    def mixed(inner, taps_ref, time_ref, own_ref, row, where):
        before = conv_row(inner, taps_ref, row, stride, masks)
        before = before.astype(jnp.bfloat16).astype(jnp.float32)
        extended = jnp.concatenate([before, own_ref[where].astype(jnp.float32)], axis=0)
        total = extended[stride:] * time_ref[0:1]
        for lag in range(1, TAPS):
            start = stride - lag * cols
            total = total + extended[start : start + stride] * time_ref[lag : lag + 1]
        return total

    def body(row, carry):
        where = pl.ds(pl.multiple_of(row * stride, stride), stride)
        value = mixed(inner_v, sv_ref, tv_ref, ov_ref, row, where)
        gate = mixed(inner_g, sg_ref, tg_ref, og_ref, row, where)
        out_ref[where] = (value * jax.nn.silu(gate)).astype(jnp.bfloat16)
        return carry

    lax.fori_loop(0, hidden_ref.shape[0] // stride, body, 0)


def on_device(
    stream_in, queries, key_rows, value_rows, w_output, w_inner, w_down, spatial_taps, temporal_taps
):
    row_count, frames, col_count, width = queries.shape
    tokens = row_count * frames * col_count
    tiles = lax.axis_size("tile")
    pair = BLOCK_F // frames
    blocks = lax.axis_size("blk") // pair
    group = pair * tiles
    per_rank = -(-HEADS // group)
    bf16 = jnp.bfloat16

    w_full = lax.all_gather(w_output, "tile", axis=0, tiled=True)

    kv = pl.pallas_call(
        local_state_kernel,
        out_shape=jax.ShapeDtypeStruct((group * per_rank, HEAD_DIM, LANES), bf16),
        in_specs=vmem_specs(2),
        out_specs=vmem_specs(1)[0],
    )(key_rows.reshape(tokens, width), value_rows.reshape(tokens, width))
    state = exchange_states(
        kv.reshape(group, per_rank, HEAD_DIM, LANES), blocks, pair, tiles
    ).reshape(group * per_rank, HEAD_DIM, LANES)
    attended = pl.pallas_call(
        attention_kernel,
        out_shape=jax.ShapeDtypeStruct((tokens, width), bf16),
        in_specs=vmem_specs(2),
        out_specs=vmem_specs(1)[0],
    )(queries.reshape(tokens, width), state)

    attn_out = jnp.dot(attended, w_full, preferred_element_type=jnp.float32)
    hidden = (stream_in.reshape(tokens, width).astype(jnp.float32) + attn_out).astype(bf16)

    chan = w_inner.shape[2]
    w_flat = w_inner.reshape(width, 2 * chan)
    space = spatial_taps.reshape(9, 2 * chan)
    time = temporal_taps.reshape(TAPS, 2 * chan)
    before = shifted(hidden, "blk", 1)
    own_all = lax.all_gather(hidden, "tile", axis=0, tiled=True)
    before_all = lax.all_gather(before, "tile", axis=0, tiled=True)

    whole = tokens * tiles
    stride = frames * col_count
    lane_block = 256
    chunk = 256
    value_blocks = chan // lane_block
    full = lambda rows: pl.BlockSpec((rows, width), lambda j: (0, 0))
    block = lambda rows: pl.BlockSpec((rows, lane_block), lambda j: (0, j))
    gate = lambda rows: pl.BlockSpec((rows, lane_block), lambda j: (0, j + value_blocks))
    inner_scratch = pltpu.VMEM((whole + 2 * stride, lane_block), bf16)
    flops = 2 * whole * width * 2 * chan
    cost = pl.CostEstimate(
        flops=flops, bytes_accessed=2 * (whole * width + 2 * width * chan), transcendentals=0
    )
    spatial = pl.pallas_call(
        functools.partial(spatial_kernel, stride, col_count, chunk),
        grid=(2 * value_blocks,),
        out_shape=jax.ShapeDtypeStruct((whole, 2 * chan), bf16),
        in_specs=[full(whole), block(width), block(9)],
        out_specs=block(whole),
        scratch_shapes=[inner_scratch],
        cost_estimate=cost,
        compiler_params=pltpu.CompilerParams(vmem_limit_bytes=40 * 2**20),
    )(own_all, w_flat, space)
    gated_out = pl.pallas_call(
        functools.partial(gated_kernel, stride, col_count, chunk),
        grid=(value_blocks,),
        out_shape=jax.ShapeDtypeStruct((whole, chan), bf16),
        in_specs=[
            full(whole), block(width), gate(width), block(9), gate(9), block(TAPS), gate(TAPS),
            block(whole), gate(whole),
        ],
        out_specs=block(whole),
        scratch_shapes=[inner_scratch, inner_scratch],
        cost_estimate=cost,
        compiler_params=pltpu.CompilerParams(vmem_limit_bytes=48 * 2**20),
    )(before_all, w_flat, w_flat, space, space, time, time, spatial, spatial)

    product = jnp.dot(gated_out, w_down, preferred_element_type=jnp.float32).astype(bf16)
    ffn_out = lax.psum_scatter(product, "tile", scatter_dimension=0, tiled=True)
    layer_out = (hidden.astype(jnp.float32) + ffn_out.astype(jnp.float32)).astype(bf16)
    return layer_out.reshape(queries.shape)


def solution(mesh):
    in_specs = (
        P("tile", "blk", None, None),
        P("tile", "blk", None, None),
        P("tile", "blk", None, None),
        P("tile", "blk", None, None),
        P("tile", None),
        P(None, None, "tile"),
        P("tile", None),
        P(None, None, None, "tile"),
        P(None, None, "tile"),
    )
    out_specs = P("tile", "blk", None, None)
    return jax.shard_map(
        on_device, mesh=mesh, in_specs=in_specs, out_specs=out_specs, check_vma=False
    )
```

```python
import functools

import jax
import jax.numpy as jnp
from jax import lax
from jax.experimental import pallas as pl
from jax.experimental.pallas import tpu as pltpu
from jax.sharding import PartitionSpec as P

HEADS = 20
HEAD_DIM = 112
TAPS = 3
BLOCK_F = 4
LANES = 128
EPS = 1e-06

MESH = pl.DeviceIdType.MESH


def vmem_specs(count):
    return [pl.BlockSpec(memory_space=pltpu.VMEM)] * count


def shifted(x, axis, by):
    peers = lax.axis_size(axis)
    pairs = [(i, i + by) for i in range(peers) if 0 <= i + by < peers]
    return lax.ppermute(x, axis, pairs)


def head_columns(head):
    return slice(head * HEAD_DIM, (head + 1) * HEAD_DIM)


def local_state_kernel(key_ref, value_ref, kv_ref):
    tokens = key_ref.shape[0]
    ones = jnp.ones((tokens, LANES - HEAD_DIM), jnp.bfloat16)
    for head in range(HEADS):
        keys = jnp.maximum(key_ref[:, head_columns(head)], 0)
        values = jnp.concatenate([value_ref[:, head_columns(head)], ones], axis=1)
        kv = lax.dot_general(
            keys, values, (((0,), (0,)), ((), ())), preferred_element_type=jnp.float32
        )
        kv_ref[head] = kv.astype(jnp.bfloat16)
    for head in range(HEADS, kv_ref.shape[0]):
        kv_ref[head] = jnp.zeros(kv_ref.shape[1:], jnp.bfloat16)


def exchange_kernel(
    blocks, pair, tiles, kv_ref, state_ref, got1, got2, total, block_send, final_send, states,
    send1, recv1, send2, recv2, send3, recv3,
):
    group = pair * tiles
    blk = lax.axis_index("blk")
    tile = lax.axis_index("tile")
    block = blk // pair
    member = blk % pair
    rank = member * tiles + tile

    def peer(step):
        other = (rank + step) % group
        return other, (block * pair + other // tiles, other % tiles)

    barrier = pltpu.get_barrier_semaphore()
    for step in range(1, group):
        pl.semaphore_signal(barrier, inc=1, device_id=peer(step)[1], device_id_type=MESH)
    for step in range(1, blocks):
        other = (block + step) % blocks
        pl.semaphore_signal(
            barrier, inc=1, device_id=(other * pair + member, tile), device_id_type=MESH
        )
    pl.semaphore_wait(barrier, group - 1 + blocks - 1)

    first = []
    for step in range(1, group):
        other, device = peer(step)
        copy = pltpu.make_async_remote_copy(
            src_ref=kv_ref.at[other], dst_ref=got1.at[step], send_sem=send1.at[step],
            recv_sem=recv1.at[step], device_id=device, device_id_type=MESH,
        )
        copy.start()
        first.append(copy)
    total[...] = kv_ref[rank].astype(jnp.float32)
    for step in range(1, group):
        first[step - 1].wait_recv()
        total[...] += got1[step].astype(jnp.float32)

    block_send[...] = total[...].astype(jnp.bfloat16)

    def later(step):
        return pltpu.make_async_remote_copy(
            src_ref=block_send, dst_ref=got2.at[step], send_sem=send2.at[step],
            recv_sem=recv2.at[step], device_id=(((block + step) % blocks) * pair + member, tile),
            device_id_type=MESH,
        )

    for step in range(1, blocks):

        @pl.when(block + step < blocks)
        def _():
            later(step).start()

    for step in range(1, blocks):

        @pl.when(block >= step)
        def _():
            later(step).wait_recv()
            total[...] += got2[step].astype(jnp.float32)

    final_send[...] = total[...].astype(jnp.bfloat16)
    third = []
    for step in range(1, group):
        copy = pltpu.make_async_remote_copy(
            src_ref=final_send, dst_ref=states.at[rank], send_sem=send3.at[step],
            recv_sem=recv3.at[step], device_id=peer(step)[1], device_id_type=MESH,
        )
        copy.start()
        third.append(copy)
    state_ref[rank] = total[...].astype(jnp.bfloat16)
    for step in range(1, group):
        third[step - 1].wait_recv()
        other = (rank + group - step) % group
        state_ref[other] = states[other]
    for step in range(1, group):
        first[step - 1].wait_send()
        third[step - 1].wait_send()
    for step in range(1, blocks):

        @pl.when(block + step < blocks)
        def _():
            later(step).wait_send()


def exchange_states(kv, blocks, pair, tiles):
    group = pair * tiles
    piece = kv.shape[1:]
    dma = pltpu.SemaphoreType.DMA
    return pl.pallas_call(
        functools.partial(exchange_kernel, blocks, pair, tiles),
        out_shape=jax.ShapeDtypeStruct(kv.shape, jnp.bfloat16),
        in_specs=vmem_specs(1),
        out_specs=vmem_specs(1)[0],
        scratch_shapes=[
            pltpu.VMEM((group,) + piece, jnp.bfloat16),
            pltpu.VMEM((blocks,) + piece, jnp.bfloat16),
            pltpu.VMEM(piece, jnp.float32),
            pltpu.VMEM(piece, jnp.bfloat16),
            pltpu.VMEM(piece, jnp.bfloat16),
            pltpu.VMEM((group,) + piece, jnp.bfloat16),
            dma((group,)),
            dma((group,)),
            dma((blocks,)),
            dma((blocks,)),
            dma((group,)),
            dma((group,)),
        ],
        compiler_params=pltpu.CompilerParams(collective_id=0, has_side_effects=True),
    )(kv)


def attention_kernel(query_ref, state_ref, out_ref):
    for head in range(HEADS):
        queries = jnp.maximum(query_ref[:, head_columns(head)], 0)
        both = jnp.dot(queries, state_ref[head], preferred_element_type=jnp.float32)
        ratio = both[:, :HEAD_DIM] / (both[:, HEAD_DIM : HEAD_DIM + 1] + EPS)
        out_ref[:, head_columns(head)] = ratio.astype(jnp.bfloat16)


def column_masks(stride, cols, width):
    col = lax.broadcasted_iota(jnp.int32, (stride, width), 0) % cols
    return col > 0, col < cols - 1


def fill_inner(hidden_ref, w_ref, inner, stride, chunk):
    tokens = hidden_ref.shape[0]
    edge = jnp.zeros((stride, inner.shape[1]), jnp.bfloat16)
    inner[:stride] = edge
    inner[stride + tokens :] = edge
    for start in range(0, tokens, chunk):
        product = jnp.dot(
            hidden_ref[start : start + chunk], w_ref[...], preferred_element_type=jnp.float32
        )
        inner[stride + start : stride + start + chunk] = jax.nn.silu(product).astype(jnp.bfloat16)


def conv_row(inner, taps_ref, row, stride, masks):
    rows = [
        inner[pl.ds(pl.multiple_of((row + a) * stride, stride), stride)].astype(jnp.float32)
        for a in range(3)
    ]
    sums = [
        sum(rows[a] * taps_ref[3 * a + b : 3 * a + b + 1] for a in range(3)) for b in range(3)
    ]
    from_left = jnp.where(masks[0], pltpu.roll(sums[0], 1, 0), 0.0)
    from_right = jnp.where(masks[1], pltpu.roll(sums[2], stride - 1, 0), 0.0)
    return sums[1] + from_left + from_right


def spatial_kernel(stride, cols, chunk, hidden_ref, w_ref, taps_ref, out_ref, inner):
    fill_inner(hidden_ref, w_ref, inner, stride, chunk)
    masks = column_masks(stride, cols, inner.shape[1])

    def body(row, carry):
        value = conv_row(inner, taps_ref, row, stride, masks)
        out_ref[pl.ds(pl.multiple_of(row * stride, stride), stride)] = value.astype(jnp.bfloat16)
        return carry

    lax.fori_loop(0, hidden_ref.shape[0] // stride, body, 0, unroll=2)


def gated_kernel(
    stride, cols, chunk, hidden_ref, wv_ref, wg_ref, sv_ref, sg_ref, tv_ref, tg_ref, ov_ref, og_ref,
    out_ref, inner_v, inner_g,
):
    fill_inner(hidden_ref, wv_ref, inner_v, stride, chunk)
    fill_inner(hidden_ref, wg_ref, inner_g, stride, chunk)
    masks = column_masks(stride, cols, inner_v.shape[1])

    def mixed(inner, taps_ref, time_ref, own_ref, row, where):
        before = conv_row(inner, taps_ref, row, stride, masks)
        before = before.astype(jnp.bfloat16).astype(jnp.float32)
        extended = jnp.concatenate([before, own_ref[where].astype(jnp.float32)], axis=0)
        total = extended[stride:] * time_ref[0:1]
        for lag in range(1, TAPS):
            start = stride - lag * cols
            total = total + extended[start : start + stride] * time_ref[lag : lag + 1]
        return total

    def body(row, carry):
        where = pl.ds(pl.multiple_of(row * stride, stride), stride)
        value = mixed(inner_v, sv_ref, tv_ref, ov_ref, row, where)
        gate = mixed(inner_g, sg_ref, tg_ref, og_ref, row, where)
        out_ref[where] = (value * jax.nn.silu(gate)).astype(jnp.bfloat16)
        return carry

    lax.fori_loop(0, hidden_ref.shape[0] // stride, body, 0)


def scatter_sum_kernel(
    rows, chunks, product_ref, hidden_ref, out_ref, got, sums, landed, send1, recv1, send2, recv2
):
    blk = lax.axis_index("blk")
    tile = lax.axis_index("tile")
    core = tile % 2
    y = tile // 2
    order = [step % rows for step in range(1, rows + 1)]

    barrier = pltpu.get_barrier_semaphore()
    pl.semaphore_signal(barrier, inc=1, device_id=(blk, y * 2 + 1 - core), device_id_type=MESH)
    for step in range(1, rows):
        pl.semaphore_signal(
            barrier, inc=1, device_id=(blk, ((y + step) % rows) * 2 + core), device_id_type=MESH
        )
    pl.semaphore_wait(barrier, rows)

    first = {}
    for step in order:
        there = (y + step) % rows
        for k in range(chunks):
            slot = step * chunks + k
            copy = pltpu.make_async_remote_copy(
                src_ref=product_ref.at[there * 2 + 1 - core, k], dst_ref=got.at[step, k],
                send_sem=send1.at[slot], recv_sem=recv1.at[slot],
                device_id=(blk, y * 2 + 1 - core), device_id_type=MESH,
            )
            copy.start()
            first[step, k] = copy
    second = {}
    for k in range(chunks):
        for step in range(1, rows):
            there = (y + step) % rows
            slot = step * chunks + k
            first[step, k].wait_recv()
            chip = product_ref[there * 2 + core, k].astype(jnp.float32) + got[step, k].astype(
                jnp.float32
            )
            sums[step, k] = chip.astype(jnp.bfloat16)
            copy = pltpu.make_async_remote_copy(
                src_ref=sums.at[step, k], dst_ref=landed.at[step, k],
                send_sem=send2.at[slot], recv_sem=recv2.at[slot],
                device_id=(blk, there * 2 + core), device_id_type=MESH,
            )
            copy.start()
            second[step, k] = copy
    for k in range(chunks):
        first[0, k].wait_recv()
        total = product_ref[tile, k].astype(jnp.float32) + got[0, k].astype(jnp.float32)
        for step in range(1, rows):
            second[step, k].wait_recv()
            total = total + landed[step, k].astype(jnp.float32)
        out_ref[k] = (hidden_ref[k].astype(jnp.float32) + total).astype(jnp.bfloat16)
    for copy in list(first.values()) + list(second.values()):
        copy.wait_send()


def scatter_sum(product, hidden, tiles):
    rows = tiles // 2
    chunks = 4
    tokens, width = hidden.shape
    piece = (chunks, tokens // chunks, width)
    bf16 = jnp.bfloat16
    sems = [pltpu.SemaphoreType.DMA((rows * chunks,))] * 4
    return pl.pallas_call(
        functools.partial(scatter_sum_kernel, rows, chunks),
        out_shape=jax.ShapeDtypeStruct(piece, bf16),
        in_specs=vmem_specs(2),
        out_specs=vmem_specs(1)[0],
        scratch_shapes=[pltpu.VMEM((rows,) + piece, bf16)] * 3 + sems,
        compiler_params=pltpu.CompilerParams(
            collective_id=1, has_side_effects=True, vmem_limit_bytes=40 * 2**20
        ),
    )(product.reshape((tiles,) + piece), hidden.reshape(piece))


def on_device(
    stream_in, queries, key_rows, value_rows, w_output, w_inner, w_down, spatial_taps, temporal_taps
):
    row_count, frames, col_count, width = queries.shape
    tokens = row_count * frames * col_count
    tiles = lax.axis_size("tile")
    pair = BLOCK_F // frames
    blocks = lax.axis_size("blk") // pair
    group = pair * tiles
    per_rank = -(-HEADS // group)
    bf16 = jnp.bfloat16

    w_full = lax.all_gather(w_output, "tile", axis=0, tiled=True)

    kv = pl.pallas_call(
        local_state_kernel,
        out_shape=jax.ShapeDtypeStruct((group * per_rank, HEAD_DIM, LANES), bf16),
        in_specs=vmem_specs(2),
        out_specs=vmem_specs(1)[0],
    )(key_rows.reshape(tokens, width), value_rows.reshape(tokens, width))
    state = exchange_states(
        kv.reshape(group, per_rank, HEAD_DIM, LANES), blocks, pair, tiles
    ).reshape(group * per_rank, HEAD_DIM, LANES)
    attended = pl.pallas_call(
        attention_kernel,
        out_shape=jax.ShapeDtypeStruct((tokens, width), bf16),
        in_specs=vmem_specs(2),
        out_specs=vmem_specs(1)[0],
    )(queries.reshape(tokens, width), state)

    attn_out = jnp.dot(attended, w_full, preferred_element_type=jnp.float32)
    hidden = (stream_in.reshape(tokens, width).astype(jnp.float32) + attn_out).astype(bf16)

    chan = w_inner.shape[2]
    w_flat = w_inner.reshape(width, 2 * chan)
    space = spatial_taps.reshape(9, 2 * chan)
    time = temporal_taps.reshape(TAPS, 2 * chan)
    before = shifted(hidden, "blk", 1)
    own_all = lax.all_gather(hidden, "tile", axis=0, tiled=True)
    before_all = lax.all_gather(before, "tile", axis=0, tiled=True)

    whole = tokens * tiles
    stride = frames * col_count
    lane_block = 256
    chunk = 256
    value_blocks = chan // lane_block
    full = lambda rows: pl.BlockSpec((rows, width), lambda j: (0, 0))
    block = lambda rows: pl.BlockSpec((rows, lane_block), lambda j: (0, j))
    gate = lambda rows: pl.BlockSpec((rows, lane_block), lambda j: (0, j + value_blocks))
    inner_scratch = pltpu.VMEM((whole + 2 * stride, lane_block), bf16)
    flops = 2 * whole * width * 2 * chan
    cost = pl.CostEstimate(
        flops=flops, bytes_accessed=2 * (whole * width + 2 * width * chan), transcendentals=0
    )
    spatial = pl.pallas_call(
        functools.partial(spatial_kernel, stride, col_count, chunk),
        grid=(2 * value_blocks,),
        out_shape=jax.ShapeDtypeStruct((whole, 2 * chan), bf16),
        in_specs=[full(whole), block(width), block(9)],
        out_specs=block(whole),
        scratch_shapes=[inner_scratch],
        cost_estimate=cost,
        compiler_params=pltpu.CompilerParams(vmem_limit_bytes=40 * 2**20),
    )(own_all, w_flat, space)
    gated_out = pl.pallas_call(
        functools.partial(gated_kernel, stride, col_count, chunk),
        grid=(value_blocks,),
        out_shape=jax.ShapeDtypeStruct((whole, chan), bf16),
        in_specs=[
            full(whole), block(width), gate(width), block(9), gate(9), block(TAPS), gate(TAPS),
            block(whole), gate(whole),
        ],
        out_specs=block(whole),
        scratch_shapes=[inner_scratch, inner_scratch],
        cost_estimate=cost,
        compiler_params=pltpu.CompilerParams(vmem_limit_bytes=48 * 2**20),
    )(before_all, w_flat, w_flat, space, space, time, time, spatial, spatial)

    product = jnp.dot(gated_out, w_down, preferred_element_type=jnp.float32).astype(bf16)
    layer_out = scatter_sum(product, hidden, tiles)
    return layer_out.reshape(queries.shape)


def solution(mesh):
    in_specs = (
        P("tile", "blk", None, None),
        P("tile", "blk", None, None),
        P("tile", "blk", None, None),
        P("tile", "blk", None, None),
        P("tile", None),
        P(None, None, "tile"),
        P("tile", None),
        P(None, None, None, "tile"),
        P(None, None, "tile"),
    )
    out_specs = P("tile", "blk", None, None)
    return jax.shard_map(
        on_device, mesh=mesh, in_specs=in_specs, out_specs=out_specs, check_vma=False
    )
```

```python
import functools

import jax
import jax.numpy as jnp
from jax import lax
from jax.experimental import pallas as pl
from jax.experimental.pallas import tpu as pltpu
from jax.sharding import PartitionSpec as P

HEADS = 20
HEAD_DIM = 112
TAPS = 3
BLOCK_F = 4
LANES = 128
EPS = 1e-06

MESH = pl.DeviceIdType.MESH


def vmem_specs(count):
    return [pl.BlockSpec(memory_space=pltpu.VMEM)] * count


def shifted(x, axis, by):
    peers = lax.axis_size(axis)
    pairs = [(i, i + by) for i in range(peers) if 0 <= i + by < peers]
    return lax.ppermute(x, axis, pairs)


def head_columns(head):
    return slice(head * HEAD_DIM, (head + 1) * HEAD_DIM)


def local_state_kernel(key_ref, value_ref, kv_ref):
    tokens = key_ref.shape[0]
    ones = jnp.ones((tokens, LANES - HEAD_DIM), jnp.bfloat16)
    for head in range(HEADS):
        keys = jnp.maximum(key_ref[:, head_columns(head)], 0)
        values = jnp.concatenate([value_ref[:, head_columns(head)], ones], axis=1)
        kv = lax.dot_general(
            keys, values, (((0,), (0,)), ((), ())), preferred_element_type=jnp.float32
        )
        kv_ref[head] = kv.astype(jnp.bfloat16)
    for head in range(HEADS, kv_ref.shape[0]):
        kv_ref[head] = jnp.zeros(kv_ref.shape[1:], jnp.bfloat16)


def exchange_kernel(
    blocks, pair, tiles, kv_ref, w_ref, state_ref, w_out, got1, got2, total, block_send, final_send,
    states, send1, recv1, send2, recv2, send3, recv3, send_w, recv_w, send_relay, recv_relay, own_w,
):
    group = pair * tiles
    blk = lax.axis_index("blk")
    tile = lax.axis_index("tile")
    block = blk // pair
    member = blk % pair
    rank = member * tiles + tile

    def peer(step):
        other = (rank + step) % group
        return other, (block * pair + other // tiles, other % tiles)

    barrier = pltpu.get_barrier_semaphore()
    for step in range(1, group):
        pl.semaphore_signal(barrier, inc=1, device_id=peer(step)[1], device_id_type=MESH)
    for step in range(1, blocks):
        other = (block + step) % blocks
        pl.semaphore_signal(
            barrier, inc=1, device_id=(other * pair + member, tile), device_id_type=MESH
        )
    pl.semaphore_wait(barrier, group - 1 + blocks - 1)

    first = []
    for step in range(1, group):
        other, device = peer(step)
        copy = pltpu.make_async_remote_copy(
            src_ref=kv_ref.at[other], dst_ref=got1.at[step], send_sem=send1.at[step],
            recv_sem=recv1.at[step], device_id=device, device_id_type=MESH,
        )
        copy.start()
        first.append(copy)

    rows = tiles // 2
    core = tile % 2
    y = tile // 2
    chunks = w_ref.shape[0]
    partner = y * 2 + 1 - core
    own = pltpu.make_async_copy(w_ref, w_out.at[tile], own_w)
    own.start()
    direct = {}
    for k in range(chunks):
        for step in range(rows):
            target = partner if step == 0 else ((y + step) % rows) * 2 + core
            direct[step, k] = pltpu.make_async_remote_copy(
                src_ref=w_ref.at[k], dst_ref=w_out.at[tile, k],
                send_sem=send_w.at[step * chunks + k], recv_sem=recv_w.at[step * chunks + k],
                device_id=(blk, target), device_id_type=MESH,
            )
            direct[step, k].start()

    total[...] = kv_ref[rank].astype(jnp.float32)
    for step in range(1, group):
        first[step - 1].wait_recv()
        total[...] += got1[step].astype(jnp.float32)

    block_send[...] = total[...].astype(jnp.bfloat16)

    def later(step):
        return pltpu.make_async_remote_copy(
            src_ref=block_send, dst_ref=got2.at[step], send_sem=send2.at[step],
            recv_sem=recv2.at[step], device_id=(((block + step) % blocks) * pair + member, tile),
            device_id_type=MESH,
        )

    for step in range(1, blocks):

        @pl.when(block + step < blocks)
        def _():
            later(step).start()

    for step in range(1, blocks):

        @pl.when(block >= step)
        def _():
            later(step).wait_recv()
            total[...] += got2[step].astype(jnp.float32)

    final_send[...] = total[...].astype(jnp.bfloat16)
    third = []
    for step in range(1, group):
        copy = pltpu.make_async_remote_copy(
            src_ref=final_send, dst_ref=states.at[rank], send_sem=send3.at[step],
            recv_sem=recv3.at[step], device_id=peer(step)[1], device_id_type=MESH,
        )
        copy.start()
        third.append(copy)
    state_ref[rank] = total[...].astype(jnp.bfloat16)
    for step in range(1, group):
        third[step - 1].wait_recv()
        other = (rank + group - step) % group
        state_ref[other] = states[other]
    for step in range(1, group):
        first[step - 1].wait_send()
        third[step - 1].wait_send()
    for step in range(1, blocks):

        @pl.when(block + step < blocks)
        def _():
            later(step).wait_send()

    relays = []
    for k in range(chunks):
        for step in range(1, rows):
            source = ((y + rows - step) % rows) * 2 + core
            direct[step, k].wait_recv()
            relay = pltpu.make_async_remote_copy(
                src_ref=w_out.at[source, k], dst_ref=w_out.at[source, k],
                send_sem=send_relay.at[step * chunks + k],
                recv_sem=recv_relay.at[step * chunks + k],
                device_id=(blk, partner), device_id_type=MESH,
            )
            relay.start()
            relays.append(relay)
    for k in range(chunks):
        direct[0, k].wait_recv()
    for relay in relays:
        relay.wait_recv()
    for copy in list(direct.values()) + relays:
        copy.wait_send()
    own.wait()


def exchange_states(kv, w, blocks, pair, tiles):
    group = pair * tiles
    piece = kv.shape[1:]
    dma = pltpu.SemaphoreType.DMA
    copies = (tiles // 2) * w.shape[0]
    return pl.pallas_call(
        functools.partial(exchange_kernel, blocks, pair, tiles),
        out_shape=(
            jax.ShapeDtypeStruct(kv.shape, jnp.bfloat16),
            jax.ShapeDtypeStruct((tiles,) + w.shape, jnp.bfloat16),
        ),
        in_specs=vmem_specs(2),
        out_specs=(vmem_specs(1)[0], pl.BlockSpec(memory_space=pl.ANY)),
        scratch_shapes=[
            pltpu.VMEM((group,) + piece, jnp.bfloat16),
            pltpu.VMEM((blocks,) + piece, jnp.bfloat16),
            pltpu.VMEM(piece, jnp.float32),
            pltpu.VMEM(piece, jnp.bfloat16),
            pltpu.VMEM(piece, jnp.bfloat16),
            pltpu.VMEM((group,) + piece, jnp.bfloat16),
            dma((group,)),
            dma((group,)),
            dma((blocks,)),
            dma((blocks,)),
            dma((group,)),
            dma((group,)),
        ]
        + [dma((copies,))] * 4
        + [dma],
        compiler_params=pltpu.CompilerParams(collective_id=0, has_side_effects=True),
    )(kv, w)


def attention_kernel(query_ref, state_ref, out_ref):
    for head in range(HEADS):
        queries = jnp.maximum(query_ref[:, head_columns(head)], 0)
        both = jnp.dot(queries, state_ref[head], preferred_element_type=jnp.float32)
        ratio = both[:, :HEAD_DIM] / (both[:, HEAD_DIM : HEAD_DIM + 1] + EPS)
        out_ref[:, head_columns(head)] = ratio.astype(jnp.bfloat16)


def column_masks(stride, cols, width):
    col = lax.broadcasted_iota(jnp.int32, (stride, width), 0) % cols
    return col > 0, col < cols - 1


def fill_inner(hidden_ref, w_ref, inner, stride, chunk):
    tokens = hidden_ref.shape[0]
    edge = jnp.zeros((stride, inner.shape[1]), jnp.bfloat16)
    inner[:stride] = edge
    inner[stride + tokens :] = edge
    for start in range(0, tokens, chunk):
        product = jnp.dot(
            hidden_ref[start : start + chunk], w_ref[...], preferred_element_type=jnp.float32
        )
        inner[stride + start : stride + start + chunk] = jax.nn.silu(product).astype(jnp.bfloat16)


def conv_row(inner, taps_ref, row, stride, masks):
    rows = [
        inner[pl.ds(pl.multiple_of((row + a) * stride, stride), stride)].astype(jnp.float32)
        for a in range(3)
    ]
    sums = [
        sum(rows[a] * taps_ref[3 * a + b : 3 * a + b + 1] for a in range(3)) for b in range(3)
    ]
    from_left = jnp.where(masks[0], pltpu.roll(sums[0], 1, 0), 0.0)
    from_right = jnp.where(masks[1], pltpu.roll(sums[2], stride - 1, 0), 0.0)
    return sums[1] + from_left + from_right


def spatial_kernel(stride, cols, chunk, hidden_ref, w_ref, taps_ref, out_ref, inner):
    fill_inner(hidden_ref, w_ref, inner, stride, chunk)
    masks = column_masks(stride, cols, inner.shape[1])

    def body(row, carry):
        value = conv_row(inner, taps_ref, row, stride, masks)
        out_ref[pl.ds(pl.multiple_of(row * stride, stride), stride)] = value.astype(jnp.bfloat16)
        return carry

    lax.fori_loop(0, hidden_ref.shape[0] // stride, body, 0, unroll=2)


def gated_kernel(
    stride, cols, chunk, hidden_ref, wv_ref, wg_ref, sv_ref, sg_ref, tv_ref, tg_ref, ov_ref, og_ref,
    out_ref, inner_v, inner_g,
):
    fill_inner(hidden_ref, wv_ref, inner_v, stride, chunk)
    fill_inner(hidden_ref, wg_ref, inner_g, stride, chunk)
    masks = column_masks(stride, cols, inner_v.shape[1])

    def mixed(inner, taps_ref, time_ref, own_ref, row, where):
        before = conv_row(inner, taps_ref, row, stride, masks)
        before = before.astype(jnp.bfloat16).astype(jnp.float32)
        extended = jnp.concatenate([before, own_ref[where].astype(jnp.float32)], axis=0)
        total = extended[stride:] * time_ref[0:1]
        for lag in range(1, TAPS):
            start = stride - lag * cols
            total = total + extended[start : start + stride] * time_ref[lag : lag + 1]
        return total

    def body(row, carry):
        where = pl.ds(pl.multiple_of(row * stride, stride), stride)
        value = mixed(inner_v, sv_ref, tv_ref, ov_ref, row, where)
        gate = mixed(inner_g, sg_ref, tg_ref, og_ref, row, where)
        out_ref[where] = (value * jax.nn.silu(gate)).astype(jnp.bfloat16)
        return carry

    lax.fori_loop(0, hidden_ref.shape[0] // stride, body, 0)


def scatter_sum_kernel(
    rows, chunks, product_ref, hidden_ref, out_ref, got, sums, landed, send1, recv1, send2, recv2
):
    blk = lax.axis_index("blk")
    tile = lax.axis_index("tile")
    core = tile % 2
    y = tile // 2
    order = [step % rows for step in range(1, rows + 1)]

    barrier = pltpu.get_barrier_semaphore()
    pl.semaphore_signal(barrier, inc=1, device_id=(blk, y * 2 + 1 - core), device_id_type=MESH)
    for step in range(1, rows):
        pl.semaphore_signal(
            barrier, inc=1, device_id=(blk, ((y + step) % rows) * 2 + core), device_id_type=MESH
        )
    pl.semaphore_wait(barrier, rows)

    first = {}
    for step in order:
        there = (y + step) % rows
        for k in range(chunks):
            slot = step * chunks + k
            copy = pltpu.make_async_remote_copy(
                src_ref=product_ref.at[there * 2 + 1 - core, k], dst_ref=got.at[step, k],
                send_sem=send1.at[slot], recv_sem=recv1.at[slot],
                device_id=(blk, y * 2 + 1 - core), device_id_type=MESH,
            )
            copy.start()
            first[step, k] = copy
    second = {}
    for k in range(chunks):
        for step in range(1, rows):
            there = (y + step) % rows
            slot = step * chunks + k
            first[step, k].wait_recv()
            chip = product_ref[there * 2 + core, k].astype(jnp.float32) + got[step, k].astype(
                jnp.float32
            )
            sums[step, k] = chip.astype(jnp.bfloat16)
            copy = pltpu.make_async_remote_copy(
                src_ref=sums.at[step, k], dst_ref=landed.at[step, k],
                send_sem=send2.at[slot], recv_sem=recv2.at[slot],
                device_id=(blk, there * 2 + core), device_id_type=MESH,
            )
            copy.start()
            second[step, k] = copy
    for k in range(chunks):
        first[0, k].wait_recv()
        total = product_ref[tile, k].astype(jnp.float32) + got[0, k].astype(jnp.float32)
        for step in range(1, rows):
            second[step, k].wait_recv()
            total = total + landed[step, k].astype(jnp.float32)
        out_ref[k] = (hidden_ref[k].astype(jnp.float32) + total).astype(jnp.bfloat16)
    for copy in list(first.values()) + list(second.values()):
        copy.wait_send()


def scatter_sum(product, hidden, tiles):
    rows = tiles // 2
    chunks = 4
    tokens, width = hidden.shape
    piece = (chunks, tokens // chunks, width)
    bf16 = jnp.bfloat16
    sems = [pltpu.SemaphoreType.DMA((rows * chunks,))] * 4
    return pl.pallas_call(
        functools.partial(scatter_sum_kernel, rows, chunks),
        out_shape=jax.ShapeDtypeStruct(piece, bf16),
        in_specs=vmem_specs(2),
        out_specs=vmem_specs(1)[0],
        scratch_shapes=[pltpu.VMEM((rows,) + piece, bf16)] * 3 + sems,
        compiler_params=pltpu.CompilerParams(
            collective_id=1, has_side_effects=True, vmem_limit_bytes=40 * 2**20
        ),
    )(product.reshape((tiles,) + piece), hidden.reshape(piece))


def on_device(
    stream_in, queries, key_rows, value_rows, w_output, w_inner, w_down, spatial_taps, temporal_taps
):
    row_count, frames, col_count, width = queries.shape
    tokens = row_count * frames * col_count
    tiles = lax.axis_size("tile")
    pair = BLOCK_F // frames
    blocks = lax.axis_size("blk") // pair
    group = pair * tiles
    per_rank = -(-HEADS // group)
    bf16 = jnp.bfloat16

    kv = pl.pallas_call(
        local_state_kernel,
        out_shape=jax.ShapeDtypeStruct((group * per_rank, HEAD_DIM, LANES), bf16),
        in_specs=vmem_specs(2),
        out_specs=vmem_specs(1)[0],
    )(key_rows.reshape(tokens, width), value_rows.reshape(tokens, width))
    state, w_full = exchange_states(
        kv.reshape(group, per_rank, HEAD_DIM, LANES), w_output.reshape(5, -1, width), blocks, pair,
        tiles,
    )
    state = state.reshape(group * per_rank, HEAD_DIM, LANES)
    w_full = w_full.reshape(width, width)
    attended = pl.pallas_call(
        attention_kernel,
        out_shape=jax.ShapeDtypeStruct((tokens, width), bf16),
        in_specs=vmem_specs(2),
        out_specs=vmem_specs(1)[0],
    )(queries.reshape(tokens, width), state)

    attn_out = jnp.dot(attended, w_full, preferred_element_type=jnp.float32)
    hidden = (stream_in.reshape(tokens, width).astype(jnp.float32) + attn_out).astype(bf16)

    chan = w_inner.shape[2]
    w_flat = w_inner.reshape(width, 2 * chan)
    space = spatial_taps.reshape(9, 2 * chan)
    time = temporal_taps.reshape(TAPS, 2 * chan)
    before = shifted(hidden, "blk", 1)
    own_all = lax.all_gather(hidden, "tile", axis=0, tiled=True)
    before_all = lax.all_gather(before, "tile", axis=0, tiled=True)

    whole = tokens * tiles
    stride = frames * col_count
    lane_block = 256
    chunk = 256
    value_blocks = chan // lane_block
    full = lambda rows: pl.BlockSpec((rows, width), lambda j: (0, 0))
    block = lambda rows: pl.BlockSpec((rows, lane_block), lambda j: (0, j))
    gate = lambda rows: pl.BlockSpec((rows, lane_block), lambda j: (0, j + value_blocks))
    inner_scratch = pltpu.VMEM((whole + 2 * stride, lane_block), bf16)
    flops = 2 * whole * width * 2 * chan
    cost = pl.CostEstimate(
        flops=flops, bytes_accessed=2 * (whole * width + 2 * width * chan), transcendentals=0
    )
    spatial = pl.pallas_call(
        functools.partial(spatial_kernel, stride, col_count, chunk),
        grid=(2 * value_blocks,),
        out_shape=jax.ShapeDtypeStruct((whole, 2 * chan), bf16),
        in_specs=[full(whole), block(width), block(9)],
        out_specs=block(whole),
        scratch_shapes=[inner_scratch],
        cost_estimate=cost,
        compiler_params=pltpu.CompilerParams(vmem_limit_bytes=40 * 2**20),
    )(own_all, w_flat, space)
    gated_out = pl.pallas_call(
        functools.partial(gated_kernel, stride, col_count, chunk),
        grid=(value_blocks,),
        out_shape=jax.ShapeDtypeStruct((whole, chan), bf16),
        in_specs=[
            full(whole), block(width), gate(width), block(9), gate(9), block(TAPS), gate(TAPS),
            block(whole), gate(whole),
        ],
        out_specs=block(whole),
        scratch_shapes=[inner_scratch, inner_scratch],
        cost_estimate=cost,
        compiler_params=pltpu.CompilerParams(vmem_limit_bytes=48 * 2**20),
    )(before_all, w_flat, w_flat, space, space, time, time, spatial, spatial)

    product = jnp.dot(gated_out, w_down, preferred_element_type=jnp.float32).astype(bf16)
    layer_out = scatter_sum(product, hidden, tiles)
    return layer_out.reshape(queries.shape)


def solution(mesh):
    in_specs = (
        P("tile", "blk", None, None),
        P("tile", "blk", None, None),
        P("tile", "blk", None, None),
        P("tile", "blk", None, None),
        P("tile", None),
        P(None, None, "tile"),
        P("tile", None),
        P(None, None, None, "tile"),
        P(None, None, "tile"),
    )
    out_specs = P("tile", "blk", None, None)
    return jax.shard_map(
        on_device, mesh=mesh, in_specs=in_specs, out_specs=out_specs, check_vma=False
    )
```

```python
import functools

import jax
import jax.numpy as jnp
from jax import lax
from jax.experimental import pallas as pl
from jax.experimental.pallas import tpu as pltpu
from jax.sharding import PartitionSpec as P

HEADS = 20
HEAD_DIM = 112
TAPS = 3
BLOCK_F = 4
LANES = 128
EPS = 1e-06

MESH = pl.DeviceIdType.MESH


def vmem_specs(count):
    return [pl.BlockSpec(memory_space=pltpu.VMEM)] * count


def shifted(x, axis, by):
    peers = lax.axis_size(axis)
    pairs = [(i, i + by) for i in range(peers) if 0 <= i + by < peers]
    return lax.ppermute(x, axis, pairs)


def head_columns(head):
    return slice(head * HEAD_DIM, (head + 1) * HEAD_DIM)


def local_state_kernel(key_ref, value_ref, kv_ref):
    tokens = key_ref.shape[0]
    ones = jnp.ones((tokens, LANES - HEAD_DIM), jnp.bfloat16)
    for head in range(HEADS):
        keys = jnp.maximum(key_ref[:, head_columns(head)], 0)
        values = jnp.concatenate([value_ref[:, head_columns(head)], ones], axis=1)
        kv = lax.dot_general(
            keys, values, (((0,), (0,)), ((), ())), preferred_element_type=jnp.float32
        )
        kv_ref[head] = kv.astype(jnp.bfloat16)
    for head in range(HEADS, kv_ref.shape[0]):
        kv_ref[head] = jnp.zeros(kv_ref.shape[1:], jnp.bfloat16)


def exchange_kernel(
    blocks, pair, tiles, kv_ref, state_ref, got1, got2, total, block_send, final_send, states,
    send1, recv1, send2, recv2, send3, recv3,
):
    group = pair * tiles
    blk = lax.axis_index("blk")
    tile = lax.axis_index("tile")
    block = blk // pair
    member = blk % pair
    rank = member * tiles + tile

    def peer(step):
        other = (rank + step) % group
        return other, (block * pair + other // tiles, other % tiles)

    barrier = pltpu.get_barrier_semaphore()
    for step in range(1, group):
        pl.semaphore_signal(barrier, inc=1, device_id=peer(step)[1], device_id_type=MESH)
    for step in range(1, blocks):
        other = (block + step) % blocks
        pl.semaphore_signal(
            barrier, inc=1, device_id=(other * pair + member, tile), device_id_type=MESH
        )
    pl.semaphore_wait(barrier, group - 1 + blocks - 1)

    first = []
    for step in range(1, group):
        other, device = peer(step)
        copy = pltpu.make_async_remote_copy(
            src_ref=kv_ref.at[other], dst_ref=got1.at[step], send_sem=send1.at[step],
            recv_sem=recv1.at[step], device_id=device, device_id_type=MESH,
        )
        copy.start()
        first.append(copy)
    total[...] = kv_ref[rank].astype(jnp.float32)
    for step in range(1, group):
        first[step - 1].wait_recv()
        total[...] += got1[step].astype(jnp.float32)

    block_send[...] = total[...].astype(jnp.bfloat16)

    def later(step):
        return pltpu.make_async_remote_copy(
            src_ref=block_send, dst_ref=got2.at[step], send_sem=send2.at[step],
            recv_sem=recv2.at[step], device_id=(((block + step) % blocks) * pair + member, tile),
            device_id_type=MESH,
        )

    for step in range(1, blocks):

        @pl.when(block + step < blocks)
        def _():
            later(step).start()

    for step in range(1, blocks):

        @pl.when(block >= step)
        def _():
            later(step).wait_recv()
            total[...] += got2[step].astype(jnp.float32)

    final_send[...] = total[...].astype(jnp.bfloat16)
    third = []
    for step in range(1, group):
        copy = pltpu.make_async_remote_copy(
            src_ref=final_send, dst_ref=states.at[rank], send_sem=send3.at[step],
            recv_sem=recv3.at[step], device_id=peer(step)[1], device_id_type=MESH,
        )
        copy.start()
        third.append(copy)
    state_ref[rank] = total[...].astype(jnp.bfloat16)
    for step in range(1, group):
        third[step - 1].wait_recv()
        other = (rank + group - step) % group
        state_ref[other] = states[other]
    for step in range(1, group):
        first[step - 1].wait_send()
        third[step - 1].wait_send()
    for step in range(1, blocks):

        @pl.when(block + step < blocks)
        def _():
            later(step).wait_send()


def exchange_states(kv, blocks, pair, tiles):
    group = pair * tiles
    piece = kv.shape[1:]
    dma = pltpu.SemaphoreType.DMA
    return pl.pallas_call(
        functools.partial(exchange_kernel, blocks, pair, tiles),
        out_shape=jax.ShapeDtypeStruct(kv.shape, jnp.bfloat16),
        in_specs=vmem_specs(1),
        out_specs=vmem_specs(1)[0],
        scratch_shapes=[
            pltpu.VMEM((group,) + piece, jnp.bfloat16),
            pltpu.VMEM((blocks,) + piece, jnp.bfloat16),
            pltpu.VMEM(piece, jnp.float32),
            pltpu.VMEM(piece, jnp.bfloat16),
            pltpu.VMEM(piece, jnp.bfloat16),
            pltpu.VMEM((group,) + piece, jnp.bfloat16),
            dma((group,)),
            dma((group,)),
            dma((blocks,)),
            dma((blocks,)),
            dma((group,)),
            dma((group,)),
        ],
        compiler_params=pltpu.CompilerParams(collective_id=0, has_side_effects=True),
    )(kv)


def attention_kernel(query_ref, state_ref, out_ref):
    for head in range(HEADS):
        queries = jnp.maximum(query_ref[:, head_columns(head)], 0)
        both = jnp.dot(queries, state_ref[head], preferred_element_type=jnp.float32)
        ratio = both[:, :HEAD_DIM] / (both[:, HEAD_DIM : HEAD_DIM + 1] + EPS)
        out_ref[:, head_columns(head)] = ratio.astype(jnp.bfloat16)


def column_masks(stride, cols, width):
    col = lax.broadcasted_iota(jnp.int32, (stride, width), 0) % cols
    return col > 0, col < cols - 1


def fill_inner(hidden_ref, w_ref, inner, stride, chunk):
    tokens = hidden_ref.shape[0]
    edge = jnp.zeros((stride, inner.shape[1]), jnp.bfloat16)
    inner[:stride] = edge
    inner[stride + tokens :] = edge
    for start in range(0, tokens, chunk):
        product = jnp.dot(
            hidden_ref[start : start + chunk], w_ref[...], preferred_element_type=jnp.float32
        )
        inner[stride + start : stride + start + chunk] = jax.nn.silu(product).astype(jnp.bfloat16)


def conv_row(inner, taps_ref, row, stride, masks):
    rows = [
        inner[pl.ds(pl.multiple_of((row + a) * stride, stride), stride)].astype(jnp.float32)
        for a in range(3)
    ]
    sums = [
        sum(rows[a] * taps_ref[3 * a + b : 3 * a + b + 1] for a in range(3)) for b in range(3)
    ]
    from_left = jnp.where(masks[0], pltpu.roll(sums[0], 1, 0), 0.0)
    from_right = jnp.where(masks[1], pltpu.roll(sums[2], stride - 1, 0), 0.0)
    return sums[1] + from_left + from_right


def spatial_kernel(stride, cols, chunk, hidden_ref, w_ref, taps_ref, out_ref, inner):
    fill_inner(hidden_ref, w_ref, inner, stride, chunk)
    masks = column_masks(stride, cols, inner.shape[1])

    def body(row, carry):
        value = conv_row(inner, taps_ref, row, stride, masks)
        out_ref[pl.ds(pl.multiple_of(row * stride, stride), stride)] = value.astype(jnp.bfloat16)
        return carry

    lax.fori_loop(0, hidden_ref.shape[0] // stride, body, 0, unroll=2)


def gated_kernel(
    stride, cols, chunk, hidden_ref, wv_ref, wg_ref, sv_ref, sg_ref, tv_ref, tg_ref, ov_ref, og_ref,
    out_ref, inner_v, inner_g,
):
    fill_inner(hidden_ref, wv_ref, inner_v, stride, chunk)
    fill_inner(hidden_ref, wg_ref, inner_g, stride, chunk)
    masks = column_masks(stride, cols, inner_v.shape[1])

    def mixed(inner, taps_ref, time_ref, own_ref, row, where):
        before = conv_row(inner, taps_ref, row, stride, masks)
        before = before.astype(jnp.bfloat16).astype(jnp.float32)
        extended = jnp.concatenate([before, own_ref[where].astype(jnp.float32)], axis=0)
        total = extended[stride:] * time_ref[0:1]
        for lag in range(1, TAPS):
            start = stride - lag * cols
            total = total + extended[start : start + stride] * time_ref[lag : lag + 1]
        return total

    def body(row, carry):
        where = pl.ds(pl.multiple_of(row * stride, stride), stride)
        value = mixed(inner_v, sv_ref, tv_ref, ov_ref, row, where)
        gate = mixed(inner_g, sg_ref, tg_ref, og_ref, row, where)
        out_ref[where] = (value * jax.nn.silu(gate)).astype(jnp.bfloat16)
        return carry

    lax.fori_loop(0, hidden_ref.shape[0] // stride, body, 0)


def scatter_sum_kernel(
    rows, chunks, product_ref, hidden_ref, out_ref, got, sums, landed, send1, recv1, send2, recv2
):
    blk = lax.axis_index("blk")
    tile = lax.axis_index("tile")
    core = tile % 2
    y = tile // 2
    order = [step % rows for step in range(1, rows + 1)]

    barrier = pltpu.get_barrier_semaphore()
    pl.semaphore_signal(barrier, inc=1, device_id=(blk, y * 2 + 1 - core), device_id_type=MESH)
    for step in range(1, rows):
        pl.semaphore_signal(
            barrier, inc=1, device_id=(blk, ((y + step) % rows) * 2 + core), device_id_type=MESH
        )
    pl.semaphore_wait(barrier, rows)

    first = {}
    for step in order:
        there = (y + step) % rows
        for k in range(chunks):
            slot = step * chunks + k
            copy = pltpu.make_async_remote_copy(
                src_ref=product_ref.at[there * 2 + 1 - core, k], dst_ref=got.at[step, k],
                send_sem=send1.at[slot], recv_sem=recv1.at[slot],
                device_id=(blk, y * 2 + 1 - core), device_id_type=MESH,
            )
            copy.start()
            first[step, k] = copy
    second = {}
    for k in range(chunks):
        for step in range(1, rows):
            there = (y + step) % rows
            slot = step * chunks + k
            first[step, k].wait_recv()
            chip = product_ref[there * 2 + core, k].astype(jnp.float32) + got[step, k].astype(
                jnp.float32
            )
            sums[step, k] = chip.astype(jnp.bfloat16)
            copy = pltpu.make_async_remote_copy(
                src_ref=sums.at[step, k], dst_ref=landed.at[step, k],
                send_sem=send2.at[slot], recv_sem=recv2.at[slot],
                device_id=(blk, there * 2 + core), device_id_type=MESH,
            )
            copy.start()
            second[step, k] = copy
    for k in range(chunks):
        first[0, k].wait_recv()
        total = product_ref[tile, k].astype(jnp.float32) + got[0, k].astype(jnp.float32)
        for step in range(1, rows):
            second[step, k].wait_recv()
            total = total + landed[step, k].astype(jnp.float32)
        out_ref[k] = (hidden_ref[k].astype(jnp.float32) + total).astype(jnp.bfloat16)
    for copy in list(first.values()) + list(second.values()):
        copy.wait_send()


def scatter_sum(product, hidden, tiles):
    rows = tiles // 2
    chunks = 4
    tokens, width = hidden.shape
    piece = (chunks, tokens // chunks, width)
    bf16 = jnp.bfloat16
    sems = [pltpu.SemaphoreType.DMA((rows * chunks,))] * 4
    return pl.pallas_call(
        functools.partial(scatter_sum_kernel, rows, chunks),
        out_shape=jax.ShapeDtypeStruct(piece, bf16),
        in_specs=vmem_specs(2),
        out_specs=vmem_specs(1)[0],
        scratch_shapes=[pltpu.VMEM((rows,) + piece, bf16)] * 3 + sems,
        compiler_params=pltpu.CompilerParams(
            collective_id=1, has_side_effects=True, vmem_limit_bytes=40 * 2**20
        ),
    )(product.reshape((tiles,) + piece), hidden.reshape(piece))


def project_kernel(x_ref, w_ref, out_ref):
    product = jnp.dot(x_ref[...], w_ref[...], preferred_element_type=jnp.float32)
    out_ref[...] = product.astype(jnp.bfloat16)


def on_device(
    stream_in, queries, key_rows, value_rows, w_output, w_inner, w_down, spatial_taps, temporal_taps
):
    row_count, frames, col_count, width = queries.shape
    tokens = row_count * frames * col_count
    tiles = lax.axis_size("tile")
    pair = BLOCK_F // frames
    blocks = lax.axis_size("blk") // pair
    group = pair * tiles
    per_rank = -(-HEADS // group)
    bf16 = jnp.bfloat16

    w_full = lax.all_gather(w_output, "tile", axis=0, tiled=True)

    kv = pl.pallas_call(
        local_state_kernel,
        out_shape=jax.ShapeDtypeStruct((group * per_rank, HEAD_DIM, LANES), bf16),
        in_specs=vmem_specs(2),
        out_specs=vmem_specs(1)[0],
    )(key_rows.reshape(tokens, width), value_rows.reshape(tokens, width))
    state = exchange_states(
        kv.reshape(group, per_rank, HEAD_DIM, LANES), blocks, pair, tiles
    ).reshape(group * per_rank, HEAD_DIM, LANES)
    attended = pl.pallas_call(
        attention_kernel,
        out_shape=jax.ShapeDtypeStruct((tokens, width), bf16),
        in_specs=vmem_specs(2),
        out_specs=vmem_specs(1)[0],
    )(queries.reshape(tokens, width), state)

    attn_out = jnp.dot(attended, w_full, preferred_element_type=jnp.float32)
    hidden = (stream_in.reshape(tokens, width).astype(jnp.float32) + attn_out).astype(bf16)

    chan = w_inner.shape[2]
    w_flat = w_inner.reshape(width, 2 * chan)
    space = spatial_taps.reshape(9, 2 * chan)
    time = temporal_taps.reshape(TAPS, 2 * chan)
    before = shifted(hidden, "blk", 1)
    own_all = lax.all_gather(hidden, "tile", axis=0, tiled=True)
    before_all = lax.all_gather(before, "tile", axis=0, tiled=True)

    whole = tokens * tiles
    stride = frames * col_count
    lane_block = 256
    chunk = 256
    value_blocks = chan // lane_block
    full = lambda rows: pl.BlockSpec((rows, width), lambda j: (0, 0))
    block = lambda rows: pl.BlockSpec((rows, lane_block), lambda j: (0, j))
    gate = lambda rows: pl.BlockSpec((rows, lane_block), lambda j: (0, j + value_blocks))
    inner_scratch = pltpu.VMEM((whole + 2 * stride, lane_block), bf16)
    flops = 2 * whole * width * 2 * chan
    cost = pl.CostEstimate(
        flops=flops, bytes_accessed=2 * (whole * width + 2 * width * chan), transcendentals=0
    )
    spatial = pl.pallas_call(
        functools.partial(spatial_kernel, stride, col_count, chunk),
        grid=(2 * value_blocks,),
        out_shape=jax.ShapeDtypeStruct((whole, 2 * chan), bf16),
        in_specs=[full(whole), block(width), block(9)],
        out_specs=block(whole),
        scratch_shapes=[inner_scratch],
        cost_estimate=cost,
        compiler_params=pltpu.CompilerParams(vmem_limit_bytes=40 * 2**20),
    )(own_all, w_flat, space)
    gated_out = pl.pallas_call(
        functools.partial(gated_kernel, stride, col_count, chunk),
        grid=(value_blocks,),
        out_shape=jax.ShapeDtypeStruct((whole, chan), bf16),
        in_specs=[
            full(whole), block(width), gate(width), block(9), gate(9), block(TAPS), gate(TAPS),
            block(whole), gate(whole),
        ],
        out_specs=block(whole),
        scratch_shapes=[inner_scratch, inner_scratch],
        cost_estimate=cost,
        compiler_params=pltpu.CompilerParams(vmem_limit_bytes=48 * 2**20),
    )(before_all, w_flat, w_flat, space, space, time, time, spatial, spatial)

    product = pl.pallas_call(
        project_kernel,
        grid=(whole // chunk,),
        out_shape=jax.ShapeDtypeStruct((whole, width), bf16),
        in_specs=[
            pl.BlockSpec((chunk, chan), lambda j: (j, 0)),
            pl.BlockSpec((chan, width), lambda j: (0, 0)),
        ],
        out_specs=pl.BlockSpec((chunk, width), lambda j: (j, 0)),
        compiler_params=pltpu.CompilerParams(vmem_limit_bytes=32 * 2**20),
    )(gated_out, w_down)
    layer_out = scatter_sum(product, hidden, tiles)
    return layer_out.reshape(queries.shape)


def solution(mesh):
    in_specs = (
        P("tile", "blk", None, None),
        P("tile", "blk", None, None),
        P("tile", "blk", None, None),
        P("tile", "blk", None, None),
        P("tile", None),
        P(None, None, "tile"),
        P("tile", None),
        P(None, None, None, "tile"),
        P(None, None, "tile"),
    )
    out_specs = P("tile", "blk", None, None)
    return jax.shard_map(
        on_device, mesh=mesh, in_specs=in_specs, out_specs=out_specs, check_vma=False
    )
```
